32 devices in a mesh: groups: 2 (over y), gx: 16 (over z, x, core).
Axes of the slice: x: 2, y: 2, z: 4, core: 2. Of those that a mesh axis runs over, the one named last changes fastest.
Arguments:
- populations: float32 [19, 32, 64, 128], P(None, ('groups', 'gx')), parts along dimension 1, may hold values from -6 to 6
- cotangent: float32 [19, 32, 64, 128], P(None, ('groups', 'gx')), parts along dimension 1, may hold values from -6 to 6
- solid_mask: int32 [32, 64, 128], P(('groups', 'gx')), parts along dimension 0, may hold values 0 or 1
- weight_in: float32 [19, 64], replicated, may hold values from -1.25 to 1.25
- weight_mid: float32 [64, 64], replicated, may hold values from -0.75 to 0.75
- weight_out: float32 [64, 19], replicated, may hold values from -0.75 to 0.75
Outputs:
- grad_populations: float32 [19, 32, 64, 128], P(None, ('groups', 'gx')), parts along dimension 1
- grad_weight_in: float32 [38, 64], P('groups'), parts along dimension 0
- grad_weight_mid: float32 [128, 64], P('groups'), parts along dimension 0
- grad_weight_out: float32 [128, 19], P('groups'), parts along dimension 0
The draws below stay inside these ranges and needn't reach their ends.
There are 2 independent parts, one for each index of `groups`. The reference program is written for one: setup_inputs(seed, part) draws one part's arguments, and reference() takes and returns one part's arrays. A program takes and returns all parts, laid end to end along the dimension named above; an argument that names none is the same for every part. Nothing has to cross between parts.
Inputs may be any that keep to these rules, and one draw needn't show every extreme that they name: `solid_mask`: 1 marks a solid voxel and 0 a fluid one.
All inputs are finite; a program needn't handle non-finite values. No bound on the sum of `solid_mask` on one device may be relied on, other than what follows from the above.
Results may differ from the reference program's by a relative error of at most 0.000071.
Values sent between devices are 32-bit elements; how exact they have to be, the bound alone decides.
A program may use at most 64 MiB of HBM per device.

```python
import jax
import jax.numpy as jnp
from jax import lax

Q = 19
HID = 64
NY = 64
NZ = 128
NX = 16


def set_ends(values, own_key, least, high):
    index_at = [jax.random.randint(jax.random.fold_in(own_key, axis), (), 0, length) for axis, length in enumerate(values.shape)]
    widest = values.shape.index(max(values.shape))
    neighbour = index_at[:widest] + [(index_at[widest] + 1) % values.shape[widest]] + index_at[widest + 1:]
    return values.at[tuple(index_at)].set(least).at[tuple(neighbour)].set(high)


def levels(key, shape, shards, smallest, high):
    level, own = 1.0, jax.random.fold_in(key, 6)
    for position, shards_of in shards:
        draws = jnp.exp(jax.random.uniform(jax.random.fold_in(own, position), (shards_of,), jnp.float32, smallest / len(shards), high / len(shards)))
        level = level * jnp.repeat(draws, shape[position] // shards_of).reshape([-1 if axis == position else 1 for axis in range(len(shape))])
    return level


def scatter_about(stream_key, shape, spread, bound, split=(), held_as=jnp.bfloat16):
    drawn = jax.random.normal(stream_key, shape, jnp.float32) * spread
    if len(split) > 0:
        drawn = levels(stream_key, shape, split, -0.22, 0.18) * drawn
    return jnp.clip(drawn, min=-bound, max=bound).astype(held_as)


def setup_inputs(seed: int = 0, part: int = 0) -> dict:
    splits = jax.random.split(jax.random.key(seed), 7)
    part_splits = jax.random.split(jax.random.fold_in(splits[6], part), 7)
    populations = scatter_about(part_splits[0], (Q, NX, NY, NZ), 1.0, 6.0, ((1, 16),), jnp.float32)
    cotangent = scatter_about(part_splits[1], (Q, NX, NY, NZ), 1.0, 6.0, ((1, 16),), jnp.float32)
    solid_mask = set_ends((jax.random.randint(part_splits[2], (NX, NY, NZ), 0, 4) < 1).astype(jnp.int32), jax.random.fold_in(part_splits[2], 1), 0, 1)
    weight_in = scatter_about(splits[3], (Q, HID), Q ** -0.5, 1.25, (), jnp.float32)
    weight_mid = scatter_about(splits[4], (HID, HID), HID ** -0.5, 0.75, (), jnp.float32)
    weight_out = scatter_about(splits[5], (HID, Q), HID ** -0.5, 0.75, (), jnp.float32)
    return dict(populations=populations, cotangent=cotangent, solid_mask=solid_mask, weight_in=weight_in, weight_mid=weight_mid, weight_out=weight_out)


precise = lax.Precision.HIGHEST
offset_first = (1, 1, 1, 1, 1, -1, -1, -1, -1, -1, 0, 0, 0, 0, 0, 0, 0, 0, 0)
offset_second = (0, 1, -1, 0, 0, 0, 1, -1, 0, 0, 0, 1, -1, 0, 0, 1, 1, -1, -1)
offset_third = (0, 0, 0, 1, -1, 0, 0, 0, 1, -1, 0, 0, 0, 1, -1, 1, -1, 1, -1)
reverse_index = (5, 7, 6, 9, 8, 0, 2, 1, 4, 3, 10, 12, 11, 14, 13, 18, 17, 16, 15)

def neighbour_links(solid_grid):
    fluid_cells = (1 - solid_grid).astype(jnp.float32)
    padded = jnp.pad(fluid_cells, ((1, 1), (0, 0), (0, 0)))
    extent = fluid_cells.shape[0]
    layers = []
    for number in range(19):
        begin = 1 - offset_first[number]
        piece = padded[begin:begin + extent]
        layers.append(jnp.roll(piece, (offset_second[number], offset_third[number]), (1, 2)))
    return jnp.stack(layers)

def permuted(values):
    return jnp.stack([values[reverse_index[number]] for number in range(19)])

def propagate(collided, link_mask):
    pulled = jnp.stack([jnp.roll(collided[number], (offset_first[number], offset_second[number], offset_third[number]), (0, 1, 2)) for number in range(19)])
    return link_mask * pulled + (1.0 - link_mask) * permuted(collided)

def propagate_back(incoming, link_mask):
    moved = link_mask * incoming
    pushed = jnp.stack([jnp.roll(moved[number], (-offset_first[number], -offset_second[number], -offset_third[number]), (0, 1, 2)) for number in range(19)])
    return pushed + permuted((1.0 - link_mask) * incoming)

def collide_flat(flattened, weight_in, weight_mid, weight_out):
    hidden_one = jnp.tanh(jnp.dot(weight_in.T, flattened, precision=precise))
    hidden_two = jnp.tanh(jnp.dot(weight_mid.T, hidden_one, precision=precise))
    return flattened + jnp.dot(weight_out.T, hidden_two, precision=precise)

def collide(populations, weight_in, weight_mid, weight_out):

    def per_slab(slab):
        return collide_flat(slab.reshape(slab.shape[0], -1), weight_in, weight_mid, weight_out).reshape(slab.shape)
    return jnp.moveaxis(lax.map(per_slab, jnp.moveaxis(populations, 1, 0)), 0, 1)

def collide_vjp(populations, grad_post, weight_in, weight_mid, weight_out):

    def per_slab(pair):
        slab, grad_slab = pair
        shaped = slab.reshape(slab.shape[0], -1)
        value, pullback = jax.vjp(collide_flat, shaped, weight_in, weight_mid, weight_out)
        grads = pullback(grad_slab.reshape(shaped.shape))
        return (grads[0].reshape(slab.shape), grads[1], grads[2], grads[3])
    results = lax.map(per_slab, (jnp.moveaxis(populations, 1, 0), jnp.moveaxis(grad_post, 1, 0)))
    return (jnp.moveaxis(results[0], 0, 1), lax.optimization_barrier(jnp.sum(results[1], 0)), lax.optimization_barrier(jnp.sum(results[2], 0)), lax.optimization_barrier(jnp.sum(results[3], 0)))

def reference(populations, cotangent, solid_mask, weight_in, weight_mid, weight_out):
    link_mask = neighbour_links(solid_mask)
    collided = collide(populations, weight_in, weight_mid, weight_out)
    middle = propagate(collided, link_mask)
    grad_post_two = propagate_back(cotangent, link_mask)
    grad_middle, grad_in_two, grad_mid_two, grad_out_two = collide_vjp(middle, grad_post_two, weight_in, weight_mid, weight_out)
    grad_post_one = propagate_back(grad_middle, link_mask)
    grad_start, grad_in_one, grad_mid_one, grad_out_one = collide_vjp(populations, grad_post_one, weight_in, weight_mid, weight_out)
    factor = float(NX * NY * NZ) ** (-0.5)
    return (grad_start, (grad_in_one + grad_in_two) * factor, (grad_mid_one + grad_mid_two) * factor, (grad_out_one + grad_out_two) * factor)
```

```python
import functools

import jax
import jax.numpy as jnp
from jax import lax
from jax.experimental import pallas as pl
from jax.experimental.pallas import tpu as pltpu
from jax.sharding import PartitionSpec as P

offset_second = (0, 1, -1, 0, 0, 0, 1, -1, 0, 0, 0, 1, -1, 0, 0, 1, 1, -1, -1)
offset_third = (0, 0, 0, 1, -1, 0, 0, 0, 1, -1, 0, 0, 0, 1, -1, 1, -1, 1, -1)
reverse_index = (5, 7, 6, 9, 8, 0, 2, 1, 4, 3, 10, 12, 11, 14, 13, 18, 17, 16, 15)

Q = 19
QP = 24
KQ = 80
ROWS = 8

f32 = jnp.float32
bf16 = jnp.bfloat16


def shifted(plane, by_y, by_z):
    if by_y:
        plane = pltpu.roll(plane, by_y % plane.shape[0], 0)
    if by_z:
        plane = pltpu.roll(plane, by_z % plane.shape[1], 1)
    return plane


def split(x):
    high = x.astype(bf16)
    return high, (x - high.astype(f32)).astype(bf16)


def dot(a, b):
    return lax.dot_general(a, b, (((1,), (0,)), ((), ())), preferred_element_type=f32)


def dot_nt(a, b):
    return lax.dot_general(a, b, (((1,), (1,)), ((), ())), preferred_element_type=f32)


def kernel(
    n, share, factor,
    pop, cot, sol, w_in, w_mid, w_out,
    out_pop, out_in, out_mid, out_out,
    X, C, S0, U, M, G, GM, S, sol_l, sol_r,
    col_l, col_r, cot_l, cot_r, gm_l, gm_r,
    H1a, H2a, D1a, D2a, Xa, H1b, H2b, D1b, D2b, Xb, GP2, GP1, Gs,
    A1, A2, A3, B1, B2, B3, tb, acc, rs, ag,
    in_sem, out_sem, sol_send, sol_recv, cot_send, cot_recv,
    col_send, col_recv, gm_send, gm_recv, rs_send, rs_recv, ag_send, ag_recv,
):
    ny, nz = X.shape[1], X.shape[2]
    hid = w_mid.shape[0]
    steps = ny // ROWS
    T = ROWS * nz
    me = lax.axis_index("gx")
    has_left, has_right = me > 0, me < n - 1
    left, right = jnp.maximum(me - 1, 0), jnp.minimum(me + 1, n - 1)

    barrier = pltpu.get_barrier_semaphore()
    for d in range(1, n):
        pl.semaphore_signal(
            barrier, inc=1, device_id={"gx": lax.rem(me + d, n)},
            device_id_type=pl.DeviceIdType.MESH,
        )

    in_x = pltpu.make_async_copy(pop, X.at[0:Q], in_sem.at[0])
    in_s = pltpu.make_async_copy(sol, S0, in_sem.at[1])
    in_c = pltpu.make_async_copy(cot, C, in_sem.at[2])
    in_x.start()
    in_s.start()
    in_c.start()

    def remote(src, dst, send, recv, device):
        return pltpu.make_async_remote_copy(
            src_ref=src, dst_ref=dst, send_sem=send, recv_sem=recv,
            device_id={"gx": device}, device_id_type=pl.DeviceIdType.MESH,
        )

    def sol_to_right():
        return remote(sol, sol_l, sol_send.at[0], sol_recv.at[0], right)

    def sol_to_left():
        return remote(sol, sol_r, sol_send.at[1], sol_recv.at[1], left)

    def cot_to_right():
        return remote(cot.at[5:10], cot_l, cot_send.at[0], cot_recv.at[0], right)

    def cot_to_left():
        return remote(cot.at[0:5], cot_r, cot_send.at[1], cot_recv.at[1], left)

    def rows_at(k):
        return pl.ds(pl.multiple_of(k * ROWS, ROWS), ROWS)

    def col_to_right(k):
        return remote(U.at[0:5, rows_at(k)], col_l.at[:, rows_at(k)], col_send.at[0, k], col_recv.at[0, k], right)

    def col_to_left(k):
        return remote(U.at[5:10, rows_at(k)], col_r.at[:, rows_at(k)], col_send.at[1, k], col_recv.at[1, k], left)

    def gm_to_right(k):
        return remote(GM.at[5:10, rows_at(k)], gm_l.at[:, rows_at(k)], gm_send.at[0, k], gm_recv.at[0, k], right)

    def gm_to_left(k):
        return remote(GM.at[0:5, rows_at(k)], gm_r.at[:, rows_at(k)], gm_send.at[1, k], gm_recv.at[1, k], left)

    def stack3(rows, period, out):
        k, m = rows.shape
        high = rows.astype(bf16).astype(f32)
        low = rows - high
        tb[...] = jnp.zeros_like(tb)
        tb[0:k, 0:m] = high
        tb[period : period + k, 0:m] = high
        tb[2 * period : 2 * period + k, 0:m] = low
        out[...] = tb[...].T[0 : out.shape[0], 0 : out.shape[1]].astype(bf16)

    def transposed(rows, keep):
        k, m = rows.shape
        tb[...] = jnp.zeros_like(tb)
        tb[0:k, 0:m] = rows
        return tb[...].T[0:keep, 0:128]

    stack3(w_in[...], QP, A1)
    stack3(w_mid[...], hid, A2)
    stack3(w_out[...], hid, A3)
    stack3(transposed(w_in[...], hid), hid, B1)
    stack3(transposed(w_mid[...], hid), hid, B2)
    stack3(transposed(w_out[...], QP), QP, B3)

    pad = jnp.zeros((QP - Q, ny, nz), f32)
    X[Q:QP] = pad
    M[Q:QP] = pad
    G[Q:QP] = pad

    @pl.when(me == 0)
    def _():
        sol_l[...] = jnp.ones_like(sol_l)
        for ref in (col_l, cot_l, gm_l):
            ref[...] = jnp.zeros_like(ref)

    @pl.when(me == n - 1)
    def _():
        sol_r[...] = jnp.ones_like(sol_r)
        for ref in (col_r, cot_r, gm_r):
            ref[...] = jnp.zeros_like(ref)

    def gather(ref, k):
        flat = ref.reshape(QP * ny, nz)
        return jnp.concatenate(
            [flat[pl.ds(k * ROWS + r, QP, stride=ny), :] for r in range(ROWS)], axis=1
        )

    def scatter(ref, k, values):
        flat = ref.reshape(QP * ny, nz)
        for r in range(ROWS):
            flat[pl.ds(k * ROWS + r, QP, stride=ny), :] = values[:, r * nz : (r + 1) * nz]

    def lanes(k):
        return pl.ds(pl.multiple_of(k * T, T), T)

    def split_q(x):
        high = x.astype(bf16).astype(f32)
        return jnp.concatenate([high, x - high, high, jnp.zeros((KQ - 3 * QP, T), f32)], axis=0).astype(bf16)

    def layer(k, stacked, weights, H, D):
        h = jnp.tanh(dot(weights[...], stacked))
        high, low = split(h)
        H[0:hid, lanes(k)] = high
        H[hid : 2 * hid, lanes(k)] = low
        D[:, lanes(k)] = 1.0 - h * h
        return jnp.concatenate([high, low, high], axis=0)

    def forward(k, src, H1, H2, D1, D2, Xs):
        x = gather(src, k)
        x3 = split_q(x)
        Xs[:, lanes(k)] = x3[0 : 2 * QP]
        h13 = layer(k, x3, A1, H1, D1)
        return x, layer(k, h13, A2, H2, D2)

    def backward(k, D1, D2):
        g = gather(G, k)
        g3 = split_q(g)
        Gs[:, lanes(k)] = g3[0 : 2 * QP]
        high, low = split(dot(B3[...], g3) * D2[:, lanes(k)])
        GP2[0:hid, lanes(k)] = high
        GP2[hid : 2 * hid, lanes(k)] = low
        p3 = jnp.concatenate([high, low, high], axis=0)
        high, low = split(dot(B2[...], p3) * D1[:, lanes(k)])
        GP1[0:hid, lanes(k)] = high
        GP1[hid : 2 * hid, lanes(k)] = low
        p3 = jnp.concatenate([high, low, high], axis=0)
        scatter(GM, k, g + dot(B1[...], p3))

    def weight_grads(H1, H2, Xs, start):
        def body(k, carry):
            m, i, o = carry
            m = m + dot_nt(H1[:, lanes(k)], GP2[:, lanes(k)])
            i = i + dot_nt(Xs[:, lanes(k)], GP1[:, lanes(k)])
            o = o + dot_nt(Gs[:, lanes(k)], H2[:, lanes(k)])
            return m, i, o

        return lax.fori_loop(0, steps, body, start)

    def propagate_back(g, from_left, from_right):
        own = S0[...] == 0
        for i in range(Q):
            o = reverse_index[i]
            if i < 5:
                src = from_right[i]
            elif i < 10:
                src = from_left[i - 5]
            else:
                src = g[i]
            moved = shifted(src, -offset_second[i], -offset_third[i])
            if i == 10:
                G[i] = g[i]
            else:
                G[i] = jnp.where(own, moved, 0.0) + jnp.where(S[o] == 0, 0.0, g[o])

    pl.semaphore_wait(barrier, n - 1)

    @pl.when(has_right)
    def _():
        sol_to_right().start()

    @pl.when(has_left)
    def _():
        sol_to_left().start()

    in_x.wait()

    def first(k, _):
        x, h23 = forward(k, X, H1a, H2a, D1a, D2a, Xa)
        scatter(U, k, x + dot(A3[...], h23))

        @pl.when(has_right)
        def _():
            col_to_right(k).start()

        @pl.when(has_left)
        def _():
            col_to_left(k).start()

        return 0

    lax.fori_loop(0, steps, first, 0)

    @pl.when(has_right)
    def _():
        cot_to_right().start()

    @pl.when(has_left)
    def _():
        cot_to_left().start()

    in_s.wait()

    @pl.when(has_left)
    def _():
        sol_to_right().wait_recv()

    @pl.when(has_right)
    def _():
        sol_to_left().wait_recv()

    for i in range(Q):
        plane = sol_l if i < 5 else sol_r if i < 10 else S0
        S[i] = shifted(plane[...], offset_second[i], offset_third[i])

    @pl.when(has_left)
    def _():
        for k in range(steps):
            col_to_right(k).wait_recv()

    @pl.when(has_right)
    def _():
        for k in range(steps):
            col_to_left(k).wait_recv()

    for i in range(Q):
        if i == 10:
            M[i] = U[i]
            continue
        src = col_l[i] if i < 5 else col_r[i - 5] if i < 10 else U[i]
        moved = shifted(src, offset_second[i], offset_third[i])
        M[i] = jnp.where(S[i] == 0, moved, U[reverse_index[i]])

    def second(k, _):
        forward(k, M, H1b, H2b, D1b, D2b, Xb)
        return 0

    lax.fori_loop(0, steps, second, 0)

    in_c.wait()

    @pl.when(has_left)
    def _():
        cot_to_right().wait_recv()

    @pl.when(has_right)
    def _():
        cot_to_left().wait_recv()

    propagate_back(C, cot_l, cot_r)

    def third(k, _):
        backward(k, D1b, D2b)

        @pl.when(has_right)
        def _():
            gm_to_right(k).start()

        @pl.when(has_left)
        def _():
            gm_to_left(k).start()

        return 0

    lax.fori_loop(0, steps, third, 0)

    zero = (jnp.zeros((2 * hid, 2 * hid), f32), jnp.zeros((2 * QP, 2 * hid), f32), jnp.zeros((2 * QP, 2 * hid), f32))
    sums = weight_grads(H1b, H2b, Xb, zero)

    @pl.when(has_left)
    def _():
        for k in range(steps):
            gm_to_right(k).wait_recv()

    @pl.when(has_right)
    def _():
        for k in range(steps):
            gm_to_left(k).wait_recv()

    propagate_back(GM, gm_l, gm_r)

    @pl.when(has_right)
    def _():
        for k in range(steps):
            gm_to_right(k).wait_send()

    @pl.when(has_left)
    def _():
        for k in range(steps):
            gm_to_left(k).wait_send()

    def fourth(k, _):
        backward(k, D1a, D2a)
        return 0

    lax.fori_loop(0, steps, fourth, 0)
    out_x = pltpu.make_async_copy(GM.at[0:Q], out_pop, out_sem.at[0])
    out_x.start()

    sum_mid, sum_in, sum_out = weight_grads(H1a, H2a, Xa, sums)

    def folded(x):
        half = x.shape[0] // 2
        x = x[0:half] + x[half:]
        return x + pltpu.roll(x, hid, 1)

    pieces = []
    for whole in (folded(sum_mid), folded(sum_in), folded(sum_out)):
        pieces += [whole[j : j + 8] for j in range(0, whole.shape[0], 8)]
    per = share // 8
    for j in range(n * per):
        piece = pieces[j] if j < len(pieces) else jnp.zeros((8, 128), f32)
        acc[j // per, (j % per) * 8 : (j % per) * 8 + 8] = piece

    def rs_copy(d):
        to = lax.rem(me + d, n)
        return remote(acc.at[to], rs.at[me], rs_send.at[d], rs_recv.at[me], to)

    def rs_arrival(d):
        source = lax.rem(me + n - d, n)
        return remote(acc.at[me], rs.at[source], rs_send.at[d], rs_recv.at[source], source)

    for d in range(1, n):
        rs_copy(d).start()
    total = acc[me]
    for d in range(1, n):
        rs_arrival(d).wait_recv()
        total = total + rs[lax.rem(me + n - d, n)]
    ag[me] = total * factor

    def ag_copy(d):
        to = lax.rem(me + d, n)
        return remote(ag.at[me], ag.at[me], ag_send.at[d], ag_recv.at[me], to)

    def ag_arrival(d):
        source = lax.rem(me + n - d, n)
        return remote(ag.at[me], ag.at[source], ag_send.at[d], ag_recv.at[source], source)

    for d in range(1, n):
        ag_copy(d).start()
    for d in range(1, n):
        ag_arrival(d).wait_recv()

    result = [ag[j // per, (j % per) * 8 : (j % per) * 8 + 8] for j in range(len(pieces))]
    count = hid // 8
    out_mid[...] = jnp.concatenate(result[0:count], axis=0)[:, 0:hid]
    out_in[...] = jnp.concatenate(result[count : count + 3], axis=0)[0:Q, 0:hid]
    last = jnp.concatenate(result[count + 3 :], axis=0)
    out_out[...] = transposed(last, 128)[0:hid, 0:Q]

    for d in range(1, n):
        rs_copy(d).wait_send()
        ag_copy(d).wait_send()

    @pl.when(has_right)
    def _():
        sol_to_right().wait_send()
        cot_to_right().wait_send()
        for k in range(steps):
            col_to_right(k).wait_send()

    @pl.when(has_left)
    def _():
        sol_to_left().wait_send()
        cot_to_left().wait_send()
        for k in range(steps):
            col_to_left(k).wait_send()

    out_x.wait()


def per_device(n, populations, cotangent, solid_mask, weight_in, weight_mid, weight_out):
    q, nx, ny, nz = populations.shape
    hid = weight_mid.shape[0]
    voxels = ny * nz
    steps = ny // ROWS
    groups_of_8 = hid // 8 + 2 * (QP // 8)
    share = 8 * -(-groups_of_8 // n)
    factor = float(nx * voxels * n) ** (-0.5)
    plane = pltpu.VMEM((ny, nz), jnp.int32)
    planes = pltpu.VMEM((QP, ny, nz), f32)
    five = pltpu.VMEM((5, ny, nz), f32)
    stack = pltpu.VMEM((2 * hid, voxels), bf16)
    slope = pltpu.VMEM((hid, voxels), f32)
    thin = pltpu.VMEM((2 * QP, voxels), bf16)
    shares = pltpu.VMEM((n, share, 128), f32)
    dma = pltpu.SemaphoreType.DMA
    grad, g_in, g_mid, g_out = pl.pallas_call(
        functools.partial(kernel, n, share, factor),
        out_shape=(
            jax.ShapeDtypeStruct((q, ny, nz), f32),
            jax.ShapeDtypeStruct(weight_in.shape, f32),
            jax.ShapeDtypeStruct(weight_mid.shape, f32),
            jax.ShapeDtypeStruct(weight_out.shape, f32),
        ),
        in_specs=[pl.BlockSpec(memory_space=pl.ANY)] * 3 + [pl.BlockSpec(memory_space=pltpu.VMEM)] * 3,
        out_specs=(pl.BlockSpec(memory_space=pl.ANY),) + (pl.BlockSpec(memory_space=pltpu.VMEM),) * 3,
        scratch_shapes=[
            planes, pltpu.VMEM((Q, ny, nz), f32), plane, planes, planes, planes, planes,
            pltpu.VMEM((Q, ny, nz), jnp.int32), plane, plane,
            five, five, five, five, five, five,
            stack, stack, slope, slope, thin,
            stack, stack, slope, slope, thin,
            stack, stack, thin,
            pltpu.VMEM((hid, KQ), bf16), pltpu.VMEM((hid, 3 * hid), bf16), pltpu.VMEM((QP, 3 * hid), bf16),
            pltpu.VMEM((QP, 3 * hid), bf16), pltpu.VMEM((hid, 3 * hid), bf16), pltpu.VMEM((hid, KQ), bf16),
            pltpu.VMEM((256, 128), f32), shares, shares, shares,
            dma((3,)), dma((1,)), dma((2,)), dma((2,)), dma((2,)), dma((2,)),
            dma((2, steps)), dma((2, steps)), dma((2, steps)), dma((2, steps)),
            dma((n,)), dma((n,)), dma((n,)), dma((n,)),
        ],
        compiler_params=pltpu.CompilerParams(
            collective_id=0, has_side_effects=True, vmem_limit_bytes=60 * 1024 * 1024
        ),
        name="lattice_backward",
    )(
        populations.reshape(q, ny, nz), cotangent.reshape(q, ny, nz), solid_mask.reshape(ny, nz),
        weight_in, weight_mid, weight_out,
    )
    return grad.reshape(populations.shape), g_in, g_mid, g_out


def solution(mesh):
    in_specs = (
        P(None, ("groups", "gx"), None, None),
        P(None, ("groups", "gx"), None, None),
        P(("groups", "gx"), None, None),
        P(),
        P(),
        P(),
    )
    out_specs = (
        P(None, ("groups", "gx"), None, None),
        P("groups", None),
        P("groups", None),
        P("groups", None),
    )
    return jax.shard_map(
        functools.partial(per_device, mesh.shape["gx"]),
        mesh=mesh, in_specs=in_specs, out_specs=out_specs, check_vma=False,
    )
```

```python
import functools

import jax
import jax.numpy as jnp
from jax import lax
from jax.experimental import pallas as pl
from jax.experimental.pallas import tpu as pltpu
from jax.sharding import PartitionSpec as P

offset_second = (0, 1, -1, 0, 0, 0, 1, -1, 0, 0, 0, 1, -1, 0, 0, 1, 1, -1, -1)
offset_third = (0, 0, 0, 1, -1, 0, 0, 0, 1, -1, 0, 0, 0, 1, -1, 1, -1, 1, -1)
reverse_index = (5, 7, 6, 9, 8, 0, 2, 1, 4, 3, 10, 12, 11, 14, 13, 18, 17, 16, 15)

Q = 19
QP = 24
KQ = 80
ROWS = 32
GAP = 8

f32 = jnp.float32
bf16 = jnp.bfloat16


def shifted(plane, by_y, by_z):
    if by_y:
        plane = pltpu.roll(plane, by_y % plane.shape[0], 0)
    if by_z:
        plane = pltpu.roll(plane, by_z % plane.shape[1], 1)
    return plane


def split(x):
    high = x.astype(bf16)
    return high, (x - high.astype(f32)).astype(bf16)


def dot(a, b):
    return lax.dot_general(a, b, (((1,), (0,)), ((), ())), preferred_element_type=f32)


def dot_nt(a, b):
    return lax.dot_general(a, b, (((1,), (1,)), ((), ())), preferred_element_type=f32)


def kernel(
    n, share, factor,
    pop, cot, sol, hbm_in, hbm_mid, hbm_out,
    out_pop, out_in, out_mid, out_out,
    w_in, w_mid, w_out, X, C, S0, U, M, G, GM, S, sol_l, sol_r,
    col_l, col_r, cot_l, cot_r, gm_l, gm_r,
    H1a, H2a, D1a, D2a, Xa, H1b, H2b, D1b, D2b, Xb, GP2, GP1, Gs,
    A1, A2, A3, B1, B2, B3, tb, acc, rs, ag,
    in_sem, out_sem, sol_send, sol_recv, cot_send, cot_recv,
    col_send, col_recv, gm_send, gm_recv, rs_send, rs_recv, ag_send, ag_recv,
):
    ny, nz = C.shape[1], C.shape[2]
    pitch = X.shape[1]
    hid = w_mid.shape[0]
    steps = ny // ROWS
    T = ROWS * nz
    me = lax.axis_index("gx")
    has_left, has_right = me > 0, me < n - 1
    left, right = jnp.maximum(me - 1, 0), jnp.minimum(me + 1, n - 1)

    barrier = pltpu.get_barrier_semaphore()
    for d in range(1, n):
        pl.semaphore_signal(
            barrier, inc=1, device_id={"gx": lax.rem(me + d, n)},
            device_id_type=pl.DeviceIdType.MESH,
        )

    w_copies = [
        pltpu.make_async_copy(a, b, in_sem.at[3 + j])
        for j, (a, b) in enumerate(((hbm_in, w_in), (hbm_mid, w_mid), (hbm_out, w_out)))
    ]
    for copy in w_copies:
        copy.start()
    in_x = pltpu.make_async_copy(pop, X.at[0:Q, 0:ny], in_sem.at[0])
    in_s = pltpu.make_async_copy(sol, S0, in_sem.at[1])
    in_c = pltpu.make_async_copy(cot, C, in_sem.at[2])
    in_x.start()
    in_s.start()
    in_c.start()

    def remote(src, dst, send, recv, device):
        return pltpu.make_async_remote_copy(
            src_ref=src, dst_ref=dst, send_sem=send, recv_sem=recv,
            device_id={"gx": device}, device_id_type=pl.DeviceIdType.MESH,
        )

    def sol_to_right():
        return remote(sol, sol_l, sol_send.at[0], sol_recv.at[0], right)

    def sol_to_left():
        return remote(sol, sol_r, sol_send.at[1], sol_recv.at[1], left)

    def cot_to_right():
        return remote(cot.at[5:10], cot_l, cot_send.at[0], cot_recv.at[0], right)

    def cot_to_left():
        return remote(cot.at[0:5], cot_r, cot_send.at[1], cot_recv.at[1], left)

    def rows_at(k):
        return pl.ds(pl.multiple_of(k * ROWS, ROWS), ROWS)

    def col_to_right(k):
        return remote(U.at[0:5, rows_at(k)], col_l.at[:, rows_at(k)], col_send.at[0, k], col_recv.at[0, k], right)

    def col_to_left(k):
        return remote(U.at[5:10, rows_at(k)], col_r.at[:, rows_at(k)], col_send.at[1, k], col_recv.at[1, k], left)

    def gm_to_right(k):
        return remote(GM.at[5:10, rows_at(k)], gm_l.at[:, rows_at(k)], gm_send.at[0, k], gm_recv.at[0, k], right)

    def gm_to_left(k):
        return remote(GM.at[0:5, rows_at(k)], gm_r.at[:, rows_at(k)], gm_send.at[1, k], gm_recv.at[1, k], left)

    def stack3(rows, period, out, tb):
        k, m = rows.shape
        high = rows.astype(bf16).astype(f32)
        low = rows - high
        tb[...] = jnp.zeros_like(tb)
        tb[0:k, 0:m] = high
        tb[period : period + k, 0:m] = high
        tb[2 * period : 2 * period + k, 0:m] = low
        out[...] = tb[...].T[0 : out.shape[0], 0 : out.shape[1]].astype(bf16)

    def transposed(rows, keep, tb):
        k, m = rows.shape
        tb[...] = jnp.zeros_like(tb)
        tb[0:k, 0:m] = rows
        return tb[...].T[0:keep, 0:128]

    for copy in w_copies:
        copy.wait()
    stack3(w_in[...], QP, A1, tb.at[0])
    stack3(w_mid[...], hid, A2, tb.at[1])
    stack3(transposed(w_out[...], hid, tb.at[2]), hid, A3, tb.at[3])

    pad = jnp.zeros((QP - Q, ny, nz), f32)
    X[Q:QP, 0:ny] = pad
    M[Q:QP, 0:ny] = pad
    G[Q:QP, 0:ny] = pad

    @pl.when(me == 0)
    def _():
        sol_l[...] = jnp.ones_like(sol_l)
        for ref in (col_l, cot_l, gm_l):
            ref[...] = jnp.zeros_like(ref)

    @pl.when(me == n - 1)
    def _():
        sol_r[...] = jnp.ones_like(sol_r)
        for ref in (col_r, cot_r, gm_r):
            ref[...] = jnp.zeros_like(ref)

    def gather(ref, k):
        flat = ref.reshape(QP * pitch, nz)
        return jnp.concatenate(
            [flat[pl.ds(k * ROWS + r, QP, stride=pitch), :] for r in range(ROWS)], axis=1
        )

    def scatter(ref, k, values):
        flat = ref.reshape(QP * pitch, nz)
        for r in range(ROWS):
            flat[pl.ds(k * ROWS + r, QP, stride=pitch), :] = values[:, r * nz : (r + 1) * nz]

    def lanes(k):
        return pl.ds(pl.multiple_of(k * T, T), T)

    def split_q(x):
        high = x.astype(bf16).astype(f32)
        return jnp.concatenate([high, x - high, high, jnp.zeros((KQ - 3 * QP, T), f32)], axis=0).astype(bf16)

    def layer(k, stacked, weights, H, D):
        h = jnp.tanh(dot(weights[...], stacked))
        high, low = split(h)
        H[0:hid, lanes(k)] = high
        H[hid : 2 * hid, lanes(k)] = low
        D[:, lanes(k)] = 1.0 - h * h
        return jnp.concatenate([high, low, high], axis=0)

    def forward(k, src, H1, H2, D1, D2, Xs):
        x = gather(src, k)
        x3 = split_q(x)
        Xs[:, lanes(k)] = x3[0 : 2 * QP]
        h13 = layer(k, x3, A1, H1, D1)
        return x, layer(k, h13, A2, H2, D2)

    def backward(k, D1, D2):
        g = gather(G, k)
        g3 = split_q(g)
        Gs[:, lanes(k)] = g3[0 : 2 * QP]
        high, low = split(dot(B3[...], g3) * D2[:, lanes(k)])
        GP2[0:hid, lanes(k)] = high
        GP2[hid : 2 * hid, lanes(k)] = low
        p3 = jnp.concatenate([high, low, high], axis=0)
        high, low = split(dot(B2[...], p3) * D1[:, lanes(k)])
        GP1[0:hid, lanes(k)] = high
        GP1[hid : 2 * hid, lanes(k)] = low
        p3 = jnp.concatenate([high, low, high], axis=0)
        return g, p3

    def weight_grads(H1, H2, Xs, start):
        def body(k, carry):
            m, i, o = carry
            m = m + dot_nt(H1[:, lanes(k)], GP2[:, lanes(k)])
            i = i + dot_nt(Xs[:, lanes(k)], GP1[:, lanes(k)])
            o = o + dot_nt(Gs[:, lanes(k)], H2[:, lanes(k)])
            return m, i, o

        return lax.fori_loop(0, steps, body, start)

    def propagate_back(g, from_left, from_right):
        own = S0[...] == 0
        for i in range(Q):
            o = reverse_index[i]
            if i < 5:
                src = from_right[i]
            elif i < 10:
                src = from_left[i - 5]
            else:
                src = g[i, 0:ny]
            moved = shifted(src, -offset_second[i], -offset_third[i])
            if i == 10:
                G[i, 0:ny] = g[i, 0:ny]
            else:
                G[i, 0:ny] = jnp.where(own, moved, 0.0) + jnp.where(S[o] == 0, 0.0, g[o, 0:ny])

    pl.semaphore_wait(barrier, n - 1)

    @pl.when(has_right)
    def _():
        sol_to_right().start()

    @pl.when(has_left)
    def _():
        sol_to_left().start()

    in_x.wait()

    def first(k, _):
        x, h23 = forward(k, X, H1a, H2a, D1a, D2a, Xa)
        scatter(U, k, x + dot(A3[...], h23))

        @pl.when(has_right)
        def _():
            col_to_right(k).start()

        @pl.when(has_left)
        def _():
            col_to_left(k).start()

        return 0

    lax.fori_loop(0, steps, first, 0)

    @pl.when(has_right)
    def _():
        cot_to_right().start()

    @pl.when(has_left)
    def _():
        cot_to_left().start()

    stack3(transposed(w_in[...], hid, tb.at[4]), hid, B1, tb.at[5])
    stack3(transposed(w_mid[...], hid, tb.at[6]), hid, B2, tb.at[7])
    stack3(w_out[...], QP, B3, tb.at[8])

    in_s.wait()

    @pl.when(has_left)
    def _():
        sol_to_right().wait_recv()

    @pl.when(has_right)
    def _():
        sol_to_left().wait_recv()

    for i in range(Q):
        plane = sol_l if i < 5 else sol_r if i < 10 else S0
        S[i] = shifted(plane[...], offset_second[i], offset_third[i])

    @pl.when(has_left)
    def _():
        for k in range(steps):
            col_to_right(k).wait_recv()

    @pl.when(has_right)
    def _():
        for k in range(steps):
            col_to_left(k).wait_recv()

    for i in range(Q):
        if i == 10:
            M[i, 0:ny] = U[i, 0:ny]
            continue
        src = col_l[i] if i < 5 else col_r[i - 5] if i < 10 else U[i, 0:ny]
        moved = shifted(src, offset_second[i], offset_third[i])
        M[i, 0:ny] = jnp.where(S[i] == 0, moved, U[reverse_index[i], 0:ny])

    def second(k, _):
        forward(k, M, H1b, H2b, D1b, D2b, Xb)
        return 0

    lax.fori_loop(0, steps, second, 0)

    in_c.wait()

    @pl.when(has_left)
    def _():
        cot_to_right().wait_recv()

    @pl.when(has_right)
    def _():
        cot_to_left().wait_recv()

    propagate_back(C, cot_l, cot_r)

    def third(k, _):
        g, p3 = backward(k, D1b, D2b)
        scatter(GM, k, g + dot(B1[...], p3))

        @pl.when(has_right)
        def _():
            gm_to_right(k).start()

        @pl.when(has_left)
        def _():
            gm_to_left(k).start()

        return 0

    lax.fori_loop(0, steps, third, 0)

    zero = (jnp.zeros((2 * hid, 2 * hid), f32), jnp.zeros((2 * QP, 2 * hid), f32), jnp.zeros((2 * QP, 2 * hid), f32))
    sums = weight_grads(H1b, H2b, Xb, zero)

    @pl.when(has_left)
    def _():
        for k in range(steps):
            gm_to_right(k).wait_recv()

    @pl.when(has_right)
    def _():
        for k in range(steps):
            gm_to_left(k).wait_recv()

    propagate_back(GM, gm_l, gm_r)

    @pl.when(has_right)
    def _():
        for k in range(steps):
            gm_to_right(k).wait_send()

    @pl.when(has_left)
    def _():
        for k in range(steps):
            gm_to_left(k).wait_send()

    def fourth(k, _):
        backward(k, D1a, D2a)
        return 0

    lax.fori_loop(0, steps, fourth, 0)

    sum_mid, sum_in, sum_out = weight_grads(H1a, H2a, Xa, sums)

    def folded(x):
        half = x.shape[0] // 2
        x = x[0:half] + x[half:]
        return x + pltpu.roll(x, hid, 1)

    pieces = []
    for whole in (folded(sum_mid), folded(sum_in), folded(sum_out)):
        pieces += [whole[j : j + 8] for j in range(0, whole.shape[0], 8)]
    per = share // 8
    for j in range(n * per):
        piece = pieces[j] if j < len(pieces) else jnp.zeros((8, 128), f32)
        acc[j // per, (j % per) * 8 : (j % per) * 8 + 8] = piece

    def rs_copy(d):
        to = lax.rem(me + d, n)
        return remote(acc.at[to], rs.at[me], rs_send.at[d], rs_recv.at[me], to)

    def rs_arrival(d):
        source = lax.rem(me + n - d, n)
        return remote(acc.at[me], rs.at[source], rs_send.at[d], rs_recv.at[source], source)

    for d in range(1, n):
        rs_copy(d).start()

    def fifth(k, _):
        rows = GP1[:, lanes(k)]
        scatter(GM, k, gather(G, k) + dot(B1[...], jnp.concatenate([rows, rows[0:hid]], axis=0)))
        return 0

    lax.fori_loop(0, steps, fifth, 0)
    out_x = pltpu.make_async_copy(GM.at[0:Q, 0:ny], out_pop, out_sem.at[0])
    out_x.start()

    total = acc[me]
    for d in range(1, n):
        rs_arrival(d).wait_recv()
        total = total + rs[lax.rem(me + n - d, n)]
    ag[me] = total * factor

    def ag_copy(d):
        to = lax.rem(me + d, n)
        return remote(ag.at[me], ag.at[me], ag_send.at[d], ag_recv.at[me], to)

    def ag_arrival(d):
        source = lax.rem(me + n - d, n)
        return remote(ag.at[me], ag.at[source], ag_send.at[d], ag_recv.at[source], source)

    for d in range(1, n):
        ag_copy(d).start()
    for d in range(1, n):
        ag_arrival(d).wait_recv()

    result = [ag[j // per, (j % per) * 8 : (j % per) * 8 + 8] for j in range(len(pieces))]
    count = hid // 8
    out_mid[...] = jnp.concatenate(result[0:count], axis=0)[:, 0:hid]
    out_in[...] = jnp.concatenate(result[count : count + 3], axis=0)[0:Q, 0:hid]
    last = jnp.concatenate(result[count + 3 :], axis=0)
    out_out[...] = last[0:Q, 0:hid]

    for d in range(1, n):
        rs_copy(d).wait_send()
        ag_copy(d).wait_send()

    @pl.when(has_right)
    def _():
        sol_to_right().wait_send()
        cot_to_right().wait_send()
        for k in range(steps):
            col_to_right(k).wait_send()

    @pl.when(has_left)
    def _():
        sol_to_left().wait_send()
        cot_to_left().wait_send()
        for k in range(steps):
            col_to_left(k).wait_send()

    out_x.wait()


def per_device(n, populations, cotangent, solid_mask, weight_in, weight_mid, weight_out):
    q, nx, ny, nz = populations.shape
    hid = weight_mid.shape[0]
    voxels = ny * nz
    steps = ny // ROWS
    groups_of_8 = hid // 8 + 2 * (QP // 8)
    share = 8 * -(-groups_of_8 // n)
    factor = float(nx * voxels * n) ** (-0.5)
    plane = pltpu.VMEM((ny, nz), jnp.int32)
    planes = pltpu.VMEM((QP, ny + GAP, nz), f32)
    five = pltpu.VMEM((5, ny, nz), f32)
    stack = pltpu.VMEM((2 * hid, voxels), bf16)
    slope = pltpu.VMEM((hid, voxels), f32)
    thin = pltpu.VMEM((2 * QP, voxels), bf16)
    shares = pltpu.VMEM((n, share, 128), f32)
    dma = pltpu.SemaphoreType.DMA
    grad, g_in, g_mid, g_out = pl.pallas_call(
        functools.partial(kernel, n, share, factor),
        out_shape=(
            jax.ShapeDtypeStruct((q, ny, nz), f32),
            jax.ShapeDtypeStruct(weight_in.shape, f32),
            jax.ShapeDtypeStruct(weight_mid.shape, f32),
            jax.ShapeDtypeStruct((q, hid), f32),
        ),
        in_specs=[pl.BlockSpec(memory_space=pl.ANY)] * 6,
        out_specs=(pl.BlockSpec(memory_space=pl.ANY),) + (pl.BlockSpec(memory_space=pltpu.VMEM),) * 3,
        scratch_shapes=[
            pltpu.VMEM((q, hid), f32), pltpu.VMEM((hid, hid), f32), pltpu.VMEM((q, hid), f32),
            planes, pltpu.VMEM((Q, ny, nz), f32), plane, planes, planes, planes, planes,
            pltpu.VMEM((Q, ny, nz), jnp.int32), plane, plane,
            five, five, five, five, five, five,
            stack, stack, slope, slope, thin,
            stack, stack, slope, slope, thin,
            stack, stack, thin,
            pltpu.VMEM((hid, KQ), bf16), pltpu.VMEM((hid, 3 * hid), bf16), pltpu.VMEM((QP, 3 * hid), bf16),
            pltpu.VMEM((QP, 3 * hid), bf16), pltpu.VMEM((hid, 3 * hid), bf16), pltpu.VMEM((hid, KQ), bf16),
            pltpu.VMEM((9, 256, 128), f32), shares, shares, shares,
            dma((6,)), dma((1,)), dma((2,)), dma((2,)), dma((2,)), dma((2,)),
            dma((2, steps)), dma((2, steps)), dma((2, steps)), dma((2, steps)),
            dma((n,)), dma((n,)), dma((n,)), dma((n,)),
        ],
        compiler_params=pltpu.CompilerParams(
            collective_id=0, has_side_effects=True, vmem_limit_bytes=60 * 1024 * 1024
        ),
        name="lattice_backward",
    )(
        populations.reshape(q, ny, nz), cotangent.reshape(q, ny, nz), solid_mask.reshape(ny, nz),
        weight_in, weight_mid, weight_out.T,
    )
    return grad.reshape(populations.shape), g_in, g_mid, g_out.T


def solution(mesh):
    in_specs = (
        P(None, ("groups", "gx"), None, None),
        P(None, ("groups", "gx"), None, None),
        P(("groups", "gx"), None, None),
        P(),
        P(),
        P(),
    )
    out_specs = (
        P(None, ("groups", "gx"), None, None),
        P("groups", None),
        P("groups", None),
        P("groups", None),
    )
    return jax.shard_map(
        functools.partial(per_device, mesh.shape["gx"]),
        mesh=mesh, in_specs=in_specs, out_specs=out_specs, check_vma=False,
    )
```

```python
import functools
import math

import jax
import jax.numpy as jnp
from jax import lax
from jax.experimental import pallas as pl
from jax.experimental.pallas import tpu as pltpu
from jax.sharding import PartitionSpec as P

offset_second = (0, 1, -1, 0, 0, 0, 1, -1, 0, 0, 0, 1, -1, 0, 0, 1, 1, -1, -1)
offset_third = (0, 0, 0, 1, -1, 0, 0, 0, 1, -1, 0, 0, 0, 1, -1, 1, -1, 1, -1)
reverse_index = (5, 7, 6, 9, 8, 0, 2, 1, 4, 3, 10, 12, 11, 14, 13, 18, 17, 16, 15)

Q = 19
QP = 24
KQ = 80
ROWS = 32
GAP = 8

f32 = jnp.float32
bf16 = jnp.bfloat16


def shifted(plane, by_y, by_z):
    if by_y:
        plane = pltpu.roll(plane, by_y % plane.shape[0], 0)
    if by_z:
        plane = pltpu.roll(plane, by_z % plane.shape[1], 1)
    return plane


def split(x):
    high = x.astype(bf16)
    return high, (x - high.astype(f32)).astype(bf16)


def dot(a, b):
    return lax.dot_general(a, b, (((1,), (0,)), ((), ())), preferred_element_type=f32)


def dot_nt(a, b):
    return lax.dot_general(a, b, (((1,), (1,)), ((), ())), preferred_element_type=f32)


def kernel(
    n, share, factor,
    pop, cot, sol, hbm_in, hbm_mid, hbm_out,
    out_pop, out_in, out_mid, out_out,
    w_in, w_mid, w_out, X, C, S0, U, M, G, GM, S, sol_l, sol_r,
    col_l, col_r, cot_l, cot_r, gm_l, gm_r,
    H1a, H2a, D1a, D2a, Xa, H1b, H2b, D1b, D2b, Xb, GP2, GP1, Gs,
    A1, A2, A3, B1, B2, B3, tb, acc, rs, across, ag,
    in_sem, out_sem, sol_send, sol_recv, cot_send, cot_recv,
    col_send, col_recv, gm_send, gm_recv, rs_send, rs_recv, ac_send, ac_recv, ag_send, ag_recv,
):
    ny, nz = C.shape[1], C.shape[2]
    pitch = X.shape[1]
    hid = w_mid.shape[0]
    steps = ny // ROWS
    T = ROWS * nz
    me = lax.axis_index("gx")
    has_left, has_right = me > 0, me < n - 1
    left, right = jnp.maximum(me - 1, 0), jnp.minimum(me + 1, n - 1)

    barrier = pltpu.get_barrier_semaphore()
    for d in range(1, n):
        pl.semaphore_signal(
            barrier, inc=1, device_id={"gx": lax.rem(me + d, n)},
            device_id_type=pl.DeviceIdType.MESH,
        )

    w_copies = [
        pltpu.make_async_copy(a, b, in_sem.at[3 + j])
        for j, (a, b) in enumerate(((hbm_in, w_in), (hbm_mid, w_mid), (hbm_out, w_out)))
    ]
    for copy in w_copies:
        copy.start()
    in_x = pltpu.make_async_copy(pop, X.at[0:Q, 0:ny], in_sem.at[0])
    in_s = pltpu.make_async_copy(sol, S0, in_sem.at[1])
    in_c = pltpu.make_async_copy(cot, C, in_sem.at[2])
    in_x.start()
    in_s.start()
    in_c.start()

    def remote(src, dst, send, recv, device):
        return pltpu.make_async_remote_copy(
            src_ref=src, dst_ref=dst, send_sem=send, recv_sem=recv,
            device_id={"gx": device}, device_id_type=pl.DeviceIdType.MESH,
        )

    def sol_to_right():
        return remote(sol, sol_l, sol_send.at[0], sol_recv.at[0], right)

    def sol_to_left():
        return remote(sol, sol_r, sol_send.at[1], sol_recv.at[1], left)

    def cot_to_right():
        return remote(cot.at[5:10], cot_l, cot_send.at[0], cot_recv.at[0], right)

    def cot_to_left():
        return remote(cot.at[0:5], cot_r, cot_send.at[1], cot_recv.at[1], left)

    def rows_at(k):
        return pl.ds(pl.multiple_of(k * ROWS, ROWS), ROWS)

    def col_to_right(k):
        return remote(U.at[0:5, rows_at(k)], col_l.at[:, rows_at(k)], col_send.at[0, k], col_recv.at[0, k], right)

    def col_to_left(k):
        return remote(U.at[5:10, rows_at(k)], col_r.at[:, rows_at(k)], col_send.at[1, k], col_recv.at[1, k], left)

    def gm_to_right(k):
        return remote(GM.at[5:10, rows_at(k)], gm_l.at[:, rows_at(k)], gm_send.at[0, k], gm_recv.at[0, k], right)

    def gm_to_left(k):
        return remote(GM.at[0:5, rows_at(k)], gm_r.at[:, rows_at(k)], gm_send.at[1, k], gm_recv.at[1, k], left)

    def stack3(rows, period, out, tb):
        k, m = rows.shape
        high = rows.astype(bf16).astype(f32)
        low = rows - high
        tb[...] = jnp.zeros_like(tb)
        tb[0:k, 0:m] = high
        tb[period : period + k, 0:m] = high
        tb[2 * period : 2 * period + k, 0:m] = low
        out[...] = tb[...].T[0 : out.shape[0], 0 : out.shape[1]].astype(bf16)

    def transposed(rows, keep, tb):
        k, m = rows.shape
        tb[...] = jnp.zeros_like(tb)
        tb[0:k, 0:m] = rows
        return tb[...].T[0:keep, 0:128]

    for copy in w_copies:
        copy.wait()
    stack3(w_in[...], QP, A1, tb.at[0])
    stack3(w_mid[...], hid, A2, tb.at[1])
    stack3(transposed(w_out[...], hid, tb.at[2]), hid, A3, tb.at[3])

    pad = jnp.zeros((QP - Q, ny, nz), f32)
    X[Q:QP, 0:ny] = pad
    M[Q:QP, 0:ny] = pad
    G[Q:QP, 0:ny] = pad

    @pl.when(me == 0)
    def _():
        sol_l[...] = jnp.ones_like(sol_l)
        for ref in (col_l, cot_l, gm_l):
            ref[...] = jnp.zeros_like(ref)

    @pl.when(me == n - 1)
    def _():
        sol_r[...] = jnp.ones_like(sol_r)
        for ref in (col_r, cot_r, gm_r):
            ref[...] = jnp.zeros_like(ref)

    def gather(ref, k):
        flat = ref.reshape(QP * pitch, nz)
        return jnp.concatenate(
            [flat[pl.ds(k * ROWS + r, QP, stride=pitch), :] for r in range(ROWS)], axis=1
        )

    def scatter(ref, k, values):
        flat = ref.reshape(QP * pitch, nz)
        for r in range(ROWS):
            flat[pl.ds(k * ROWS + r, QP, stride=pitch), :] = values[:, r * nz : (r + 1) * nz]

    def lanes(k):
        return pl.ds(pl.multiple_of(k * T, T), T)

    def split_q(x):
        high = x.astype(bf16).astype(f32)
        return jnp.concatenate([high, x - high, high, jnp.zeros((KQ - 3 * QP, T), f32)], axis=0).astype(bf16)

    def layer(k, stacked, weights, H, D):
        h = jnp.tanh(dot(weights[...], stacked))
        high, low = split(h)
        H[0:hid, lanes(k)] = high
        H[hid : 2 * hid, lanes(k)] = low
        D[:, lanes(k)] = 1.0 - h * h
        return jnp.concatenate([high, low, high], axis=0)

    def forward(k, src, H1, H2, D1, D2, Xs):
        x = gather(src, k)
        x3 = split_q(x)
        Xs[:, lanes(k)] = x3[0 : 2 * QP]
        h13 = layer(k, x3, A1, H1, D1)
        return x, layer(k, h13, A2, H2, D2)

    def backward(k, D1, D2):
        g = gather(G, k)
        g3 = split_q(g)
        Gs[:, lanes(k)] = g3[0 : 2 * QP]
        high, low = split(dot(B3[...], g3) * D2[:, lanes(k)])
        GP2[0:hid, lanes(k)] = high
        GP2[hid : 2 * hid, lanes(k)] = low
        p3 = jnp.concatenate([high, low, high], axis=0)
        high, low = split(dot(B2[...], p3) * D1[:, lanes(k)])
        GP1[0:hid, lanes(k)] = high
        GP1[hid : 2 * hid, lanes(k)] = low
        p3 = jnp.concatenate([high, low, high], axis=0)
        return g, p3

    def weight_grads(H1, H2, Xs, start):
        def body(k, carry):
            m, i, o = carry
            m = m + dot_nt(H1[:, lanes(k)], GP2[:, lanes(k)])
            i = i + dot_nt(Xs[:, lanes(k)], GP1[:, lanes(k)])
            o = o + dot_nt(Gs[:, lanes(k)], H2[:, lanes(k)])
            return m, i, o

        return lax.fori_loop(0, steps, body, start)

    def propagate_back(g, from_left, from_right):
        own = S0[...] == 0
        for i in range(Q):
            o = reverse_index[i]
            if i < 5:
                src = from_right[i]
            elif i < 10:
                src = from_left[i - 5]
            else:
                src = g[i, 0:ny]
            moved = shifted(src, -offset_second[i], -offset_third[i])
            if i == 10:
                G[i, 0:ny] = g[i, 0:ny]
            else:
                G[i, 0:ny] = jnp.where(own, moved, 0.0) + jnp.where(S[o] == 0, 0.0, g[o, 0:ny])

    in_x.wait()

    def first(k):
        x, h23 = forward(k, X, H1a, H2a, D1a, D2a, Xa)
        scatter(U, k, x + dot(A3[...], h23))

        if k == 0:
            pl.semaphore_wait(barrier, n - 1)

            @pl.when(has_right)
            def _():
                sol_to_right().start()

            @pl.when(has_left)
            def _():
                sol_to_left().start()

        @pl.when(has_right)
        def _():
            col_to_right(k).start()

        @pl.when(has_left)
        def _():
            col_to_left(k).start()

    for k in range(steps):
        first(k)

    @pl.when(has_right)
    def _():
        cot_to_right().start()

    @pl.when(has_left)
    def _():
        cot_to_left().start()

    stack3(transposed(w_in[...], hid, tb.at[4]), hid, B1, tb.at[5])
    stack3(transposed(w_mid[...], hid, tb.at[6]), hid, B2, tb.at[7])
    stack3(w_out[...], QP, B3, tb.at[8])

    in_s.wait()

    @pl.when(has_left)
    def _():
        sol_to_right().wait_recv()

    @pl.when(has_right)
    def _():
        sol_to_left().wait_recv()

    for i in range(Q):
        plane = sol_l if i < 5 else sol_r if i < 10 else S0
        S[i] = shifted(plane[...], offset_second[i], offset_third[i])

    @pl.when(has_left)
    def _():
        for k in range(steps):
            col_to_right(k).wait_recv()

    @pl.when(has_right)
    def _():
        for k in range(steps):
            col_to_left(k).wait_recv()

    for i in range(Q):
        if i == 10:
            M[i, 0:ny] = U[i, 0:ny]
            continue
        src = col_l[i] if i < 5 else col_r[i - 5] if i < 10 else U[i, 0:ny]
        moved = shifted(src, offset_second[i], offset_third[i])
        M[i, 0:ny] = jnp.where(S[i] == 0, moved, U[reverse_index[i], 0:ny])

    def second(k, _):
        forward(k, M, H1b, H2b, D1b, D2b, Xb)
        return 0

    lax.fori_loop(0, steps, second, 0)

    in_c.wait()

    @pl.when(has_left)
    def _():
        cot_to_right().wait_recv()

    @pl.when(has_right)
    def _():
        cot_to_left().wait_recv()

    propagate_back(C, cot_l, cot_r)

    def third(k, _):
        g, p3 = backward(k, D1b, D2b)
        scatter(GM, k, g + dot(B1[...], p3))

        @pl.when(has_right)
        def _():
            gm_to_right(k).start()

        @pl.when(has_left)
        def _():
            gm_to_left(k).start()

        return 0

    lax.fori_loop(0, steps, third, 0)

    zero = (jnp.zeros((2 * hid, 2 * hid), f32), jnp.zeros((2 * QP, 2 * hid), f32), jnp.zeros((2 * QP, 2 * hid), f32))
    sums = weight_grads(H1b, H2b, Xb, zero)

    @pl.when(has_left)
    def _():
        for k in range(steps):
            gm_to_right(k).wait_recv()

    @pl.when(has_right)
    def _():
        for k in range(steps):
            gm_to_left(k).wait_recv()

    propagate_back(GM, gm_l, gm_r)

    @pl.when(has_right)
    def _():
        for k in range(steps):
            gm_to_right(k).wait_send()

    @pl.when(has_left)
    def _():
        for k in range(steps):
            gm_to_left(k).wait_send()

    def fourth(k, _):
        backward(k, D1a, D2a)
        return 0

    lax.fori_loop(0, steps, fourth, 0)

    sum_mid, sum_in, sum_out = weight_grads(H1a, H2a, Xa, sums)

    def folded(x):
        half = x.shape[0] // 2
        x = x[0:half] + x[half:]
        return x + pltpu.roll(x, hid, 1)

    pieces = []
    for whole in (folded(sum_mid), folded(sum_in), folded(sum_out)):
        pieces += [whole[j : j + 8] for j in range(0, whole.shape[0], 8)]
    per = share // 8
    for j in range(acc.shape[0] * per):
        piece = pieces[j] if j < len(pieces) else jnp.zeros((8, 128), f32)
        acc[j // per, (j % per) * 8 : (j % per) * 8 + 8] = piece

    inner = acc.shape[0]
    outer = n // inner
    mine, group = lax.rem(me, inner), me // inner
    first_of_group = group * inner

    def rs_copy(d):
        to = lax.rem(mine + d, inner)
        return remote(acc.at[to], rs.at[mine], rs_send.at[d], rs_recv.at[mine], first_of_group + to)

    def rs_arrival(d):
        source = lax.rem(mine + inner - d, inner)
        return remote(acc.at[mine], rs.at[source], rs_send.at[d], rs_recv.at[source], first_of_group + source)

    for d in range(1, inner):
        rs_copy(d).start()

    def fifth(k, _):
        rows = GP1[:, lanes(k)]
        scatter(GM, k, gather(G, k) + dot(B1[...], jnp.concatenate([rows, rows[0:hid]], axis=0)))
        return 0

    lax.fori_loop(0, steps, fifth, 0)
    out_x = pltpu.make_async_copy(GM.at[0:Q, 0:ny], out_pop, out_sem.at[0])
    out_x.start()

    total = acc[mine]
    for d in range(1, inner):
        rs_arrival(d).wait_recv()
        total = total + rs[lax.rem(mine + inner - d, inner)]
    across[group] = total

    def ac_copy(d):
        to = lax.rem(group + d, outer) * inner + mine
        return remote(across.at[group], across.at[group], ac_send.at[d], ac_recv.at[group], to)

    def ac_arrival(d):
        source = lax.rem(group + outer - d, outer)
        return remote(across.at[group], across.at[source], ac_send.at[d], ac_recv.at[source], source * inner + mine)

    for d in range(1, outer):
        ac_copy(d).start()
    for d in range(1, outer):
        ac_arrival(d).wait_recv()
    total = across[0]
    for j in range(1, outer):
        total = total + across[j]
    ag[mine] = total * factor

    def ag_copy(d):
        to = first_of_group + lax.rem(mine + d, inner)
        return remote(ag.at[mine], ag.at[mine], ag_send.at[d], ag_recv.at[mine], to)

    def ag_arrival(d):
        source = lax.rem(mine + inner - d, inner)
        return remote(ag.at[mine], ag.at[source], ag_send.at[d], ag_recv.at[source], first_of_group + source)

    for d in range(1, inner):
        ag_copy(d).start()
    for d in range(1, inner):
        ag_arrival(d).wait_recv()

    result = [ag[j // per, (j % per) * 8 : (j % per) * 8 + 8] for j in range(len(pieces))]
    count = hid // 8
    out_mid[...] = jnp.concatenate(result[0:count], axis=0)[:, 0:hid]
    out_in[...] = jnp.concatenate(result[count : count + 3], axis=0)[0:Q, 0:hid]
    last = jnp.concatenate(result[count + 3 :], axis=0)
    out_out[...] = last[0:Q, 0:hid]

    for d in range(1, inner):
        rs_copy(d).wait_send()
        ag_copy(d).wait_send()
    for d in range(1, outer):
        ac_copy(d).wait_send()

    @pl.when(has_right)
    def _():
        sol_to_right().wait_send()
        cot_to_right().wait_send()
        for k in range(steps):
            col_to_right(k).wait_send()

    @pl.when(has_left)
    def _():
        sol_to_left().wait_send()
        cot_to_left().wait_send()
        for k in range(steps):
            col_to_left(k).wait_send()

    out_x.wait()


def hand_on(*refs):
    n = (len(refs) - 2) // 3
    sources, targets, held = refs[:n], refs[n : 2 * n], refs[2 * n : 3 * n]
    in_sem, out_sem = refs[3 * n :]
    parts = [(sources[j], held[j], targets[j]) for j in range(1, n)]
    q = sources[0].shape[0]
    for at in range(0, q, 5):
        rows = pl.ds(at, min(5, q - at))
        parts.append((sources[0].at[rows], held[0].at[rows], targets[0].at[rows]))
    copies = [
        (pltpu.make_async_copy(a, b, in_sem.at[j]), pltpu.make_async_copy(b, c, out_sem.at[j]))
        for j, (a, b, c) in enumerate(parts)
    ]
    for one, _ in copies:
        one.start()
    for one, two in copies:
        one.wait()
        two.start()
    for _, two in copies:
        two.wait()


def per_device(n, populations, cotangent, solid_mask, weight_in, weight_mid, weight_out):
    q, nx, ny, nz = populations.shape
    hid = weight_mid.shape[0]
    voxels = ny * nz
    steps = ny // ROWS
    groups_of_8 = hid // 8 + 2 * (QP // 8)
    inner = math.gcd(n, 4)
    outer = n // inner
    share = 8 * -(-groups_of_8 // inner)
    factor = float(nx * voxels * n) ** (-0.5)
    plane = pltpu.VMEM((ny, nz), jnp.int32)
    planes = pltpu.VMEM((QP, ny + GAP, nz), f32)
    five = pltpu.VMEM((5, ny, nz), f32)
    stack = pltpu.VMEM((2 * hid, voxels), bf16)
    slope = pltpu.VMEM((hid, voxels), f32)
    thin = pltpu.VMEM((2 * QP, voxels), bf16)
    shares = pltpu.VMEM((inner, share, 128), f32)
    dma = pltpu.SemaphoreType.DMA
    grad, g_in, g_mid, g_out = pl.pallas_call(
        functools.partial(kernel, n, share, factor),
        out_shape=(
            jax.ShapeDtypeStruct((q, ny, nz), f32),
            jax.ShapeDtypeStruct(weight_in.shape, f32),
            jax.ShapeDtypeStruct(weight_mid.shape, f32),
            jax.ShapeDtypeStruct((q, hid), f32),
        ),
        in_specs=[pl.BlockSpec(memory_space=pl.ANY)] * 6,
        out_specs=(pl.BlockSpec(memory_space=pl.ANY),) + (pl.BlockSpec(memory_space=pltpu.VMEM),) * 3,
        scratch_shapes=[
            pltpu.VMEM((q, hid), f32), pltpu.VMEM((hid, hid), f32), pltpu.VMEM((q, hid), f32),
            planes, pltpu.VMEM((Q, ny, nz), f32), plane, planes, planes, planes, planes,
            pltpu.VMEM((Q, ny, nz), jnp.int32), plane, plane,
            five, five, five, five, five, five,
            stack, stack, slope, slope, thin,
            stack, stack, slope, slope, thin,
            stack, stack, thin,
            pltpu.VMEM((hid, KQ), bf16), pltpu.VMEM((hid, 3 * hid), bf16), pltpu.VMEM((QP, 3 * hid), bf16),
            pltpu.VMEM((QP, 3 * hid), bf16), pltpu.VMEM((hid, 3 * hid), bf16), pltpu.VMEM((hid, KQ), bf16),
            pltpu.VMEM((9, 256, 128), f32), shares, shares, pltpu.VMEM((outer, share, 128), f32), shares,
            dma((6,)), dma((1,)), dma((2,)), dma((2,)), dma((2,)), dma((2,)),
            dma((2, steps)), dma((2, steps)), dma((2, steps)), dma((2, steps)),
            dma((inner,)), dma((inner,)), dma((outer,)), dma((outer,)), dma((inner,)), dma((inner,)),
        ],
        compiler_params=pltpu.CompilerParams(
            collective_id=0, has_side_effects=True, vmem_limit_bytes=60 * 1024 * 1024
        ),
        name="lattice_backward",
    )(
        populations.reshape(q, ny, nz), cotangent.reshape(q, ny, nz), solid_mask.reshape(ny, nz),
        weight_in, weight_mid, weight_out.T,
    )
    results = (grad, g_in, g_mid, g_out)
    copies = len(results) - 1 + -(-q // 5)
    grad, g_in, g_mid, g_out = pl.pallas_call(
        hand_on,
        out_shape=tuple(jax.ShapeDtypeStruct(r.shape, r.dtype) for r in results),
        in_specs=[pl.BlockSpec(memory_space=pl.ANY)] * 4,
        out_specs=(pl.BlockSpec(memory_space=pl.ANY),) * 4,
        scratch_shapes=[pltpu.VMEM(r.shape, r.dtype) for r in results] + [dma((copies,)), dma((copies,))],
        name="hand_on",
    )(*results)
    return grad.reshape(populations.shape), g_in, g_mid, g_out.T


def solution(mesh):
    in_specs = (
        P(None, ("groups", "gx"), None, None),
        P(None, ("groups", "gx"), None, None),
        P(("groups", "gx"), None, None),
        P(),
        P(),
        P(),
    )
    out_specs = (
        P(None, ("groups", "gx"), None, None),
        P("groups", None),
        P("groups", None),
        P("groups", None),
    )
    return jax.shard_map(
        functools.partial(per_device, mesh.shape["gx"]),
        mesh=mesh, in_specs=in_specs, out_specs=out_specs, check_vma=False,
    )
```

```python
import functools
import math

import jax
import jax.numpy as jnp
from jax import lax
from jax.experimental import pallas as pl
from jax.experimental.pallas import tpu as pltpu
from jax.sharding import PartitionSpec as P

offset_second = (0, 1, -1, 0, 0, 0, 1, -1, 0, 0, 0, 1, -1, 0, 0, 1, 1, -1, -1)
offset_third = (0, 0, 0, 1, -1, 0, 0, 0, 1, -1, 0, 0, 0, 1, -1, 1, -1, 1, -1)
reverse_index = (5, 7, 6, 9, 8, 0, 2, 1, 4, 3, 10, 12, 11, 14, 13, 18, 17, 16, 15)

Q = 19
QP = 24
KQ = 80
ROWS = 32
GAP = 8

f32 = jnp.float32
bf16 = jnp.bfloat16


def shifted(plane, by_y, by_z):
    if by_y:
        plane = pltpu.roll(plane, by_y % plane.shape[0], 0)
    if by_z:
        plane = pltpu.roll(plane, by_z % plane.shape[1], 1)
    return plane


def split(x):
    high = x.astype(bf16)
    return high, (x - high.astype(f32)).astype(bf16)


def dot(a, b):
    return lax.dot_general(a, b, (((1,), (0,)), ((), ())), preferred_element_type=f32)


def dot_nt(a, b):
    return lax.dot_general(a, b, (((1,), (1,)), ((), ())), preferred_element_type=f32)


def kernel(
    n, share, factor,
    pop, cot, sol, hbm_in, hbm_mid, hbm_out,
    out_pop, out_in, out_mid, out_out,
    w_in, w_mid, w_out, X, C, S0, U, M, G, GM, S, sol_l, sol_r,
    col_l, col_r, cot_l, cot_r, gm_l, gm_r,
    H1a, H2a, D1a, D2a, Xa, H1b, H2b, D1b, D2b, Xb, GP2, GP1, Gs,
    A1, A2, A3, B1, B2, B3, tb, acc, rs, across, ag,
    in_sem, out_sem, sol_send, sol_recv, cot_send, cot_recv,
    col_send, col_recv, gm_send, gm_recv, rs_send, rs_recv, ac_send, ac_recv, ag_send, ag_recv,
):
    ny, nz = C.shape[1], C.shape[2]
    pitch = X.shape[1]
    hid = w_mid.shape[0]
    steps = ny // ROWS
    T = ROWS * nz
    me = lax.axis_index("gx")
    has_left, has_right = me > 0, me < n - 1
    left, right = jnp.maximum(me - 1, 0), jnp.minimum(me + 1, n - 1)

    barrier = pltpu.get_barrier_semaphore()
    for d in range(1, n):
        pl.semaphore_signal(
            barrier, inc=1, device_id={"gx": lax.rem(me + d, n)},
            device_id_type=pl.DeviceIdType.MESH,
        )

    w_copies = [
        pltpu.make_async_copy(a, b, in_sem.at[3 + j])
        for j, (a, b) in enumerate(((hbm_in, w_in), (hbm_mid, w_mid), (hbm_out, w_out)))
    ]
    for copy in w_copies:
        copy.start()
    in_x = pltpu.make_async_copy(pop, X.at[0:Q, 0:ny], in_sem.at[0])
    in_s = pltpu.make_async_copy(sol, S0, in_sem.at[1])
    in_c = pltpu.make_async_copy(cot, C, in_sem.at[2])
    in_x.start()
    in_s.start()
    in_c.start()

    def remote(src, dst, send, recv, device):
        return pltpu.make_async_remote_copy(
            src_ref=src, dst_ref=dst, send_sem=send, recv_sem=recv,
            device_id={"gx": device}, device_id_type=pl.DeviceIdType.MESH,
        )

    def sol_to_right():
        return remote(sol, sol_l, sol_send.at[0], sol_recv.at[0], right)

    def sol_to_left():
        return remote(sol, sol_r, sol_send.at[1], sol_recv.at[1], left)

    def cot_to_right():
        return remote(cot.at[5:10], cot_l, cot_send.at[0], cot_recv.at[0], right)

    def cot_to_left():
        return remote(cot.at[0:5], cot_r, cot_send.at[1], cot_recv.at[1], left)

    def rows_at(k):
        return pl.ds(pl.multiple_of(k * ROWS, ROWS), ROWS)

    def col_to_right(k):
        return remote(U.at[0:5, rows_at(k)], col_l.at[:, rows_at(k)], col_send.at[0, k], col_recv.at[0, k], right)

    def col_to_left(k):
        return remote(U.at[5:10, rows_at(k)], col_r.at[:, rows_at(k)], col_send.at[1, k], col_recv.at[1, k], left)

    def gm_to_right(k):
        return remote(GM.at[5:10, rows_at(k)], gm_l.at[:, rows_at(k)], gm_send.at[0, k], gm_recv.at[0, k], right)

    def gm_to_left(k):
        return remote(GM.at[0:5, rows_at(k)], gm_r.at[:, rows_at(k)], gm_send.at[1, k], gm_recv.at[1, k], left)

    def stack3(rows, period, out, tb):
        k, m = rows.shape
        high = rows.astype(bf16).astype(f32)
        low = rows - high
        tb[...] = jnp.zeros_like(tb)
        tb[0:k, 0:m] = high
        tb[period : period + k, 0:m] = high
        tb[2 * period : 2 * period + k, 0:m] = low
        out[...] = tb[...].T[0 : out.shape[0], 0 : out.shape[1]].astype(bf16)

    def transposed(rows, keep, tb):
        k, m = rows.shape
        tb[...] = jnp.zeros_like(tb)
        tb[0:k, 0:m] = rows
        return tb[...].T[0:keep, 0:128]

    for copy in w_copies:
        copy.wait()
    stack3(w_in[...], QP, A1, tb.at[0])
    stack3(w_mid[...], hid, A2, tb.at[1])
    stack3(transposed(w_out[...], hid, tb.at[2]), hid, A3, tb.at[3])

    pad = jnp.zeros((QP - Q, ny, nz), f32)
    X[Q:QP, 0:ny] = pad
    M[Q:QP, 0:ny] = pad
    G[Q:QP, 0:ny] = pad

    @pl.when(me == 0)
    def _():
        sol_l[...] = jnp.ones_like(sol_l)
        for ref in (col_l, cot_l, gm_l):
            ref[...] = jnp.zeros_like(ref)

    @pl.when(me == n - 1)
    def _():
        sol_r[...] = jnp.ones_like(sol_r)
        for ref in (col_r, cot_r, gm_r):
            ref[...] = jnp.zeros_like(ref)

    def gather(ref, k):
        flat = ref.reshape(QP * pitch, nz)
        return jnp.concatenate(
            [flat[pl.ds(k * ROWS + r, QP, stride=pitch), :] for r in range(ROWS)], axis=1
        )

    def scatter(ref, k, values):
        flat = ref.reshape(QP * pitch, nz)
        for r in range(ROWS):
            flat[pl.ds(k * ROWS + r, QP, stride=pitch), :] = values[:, r * nz : (r + 1) * nz]

    def lanes(k):
        return pl.ds(pl.multiple_of(k * T, T), T)

    def split_q(x):
        high = x.astype(bf16).astype(f32)
        return jnp.concatenate([high, x - high, high, jnp.zeros((KQ - 3 * QP, T), f32)], axis=0).astype(bf16)

    def layer(k, stacked, weights, H, D):
        h = jnp.tanh(dot(weights[...], stacked))
        high, low = split(h)
        H[0:hid, lanes(k)] = high
        H[hid : 2 * hid, lanes(k)] = low
        D[:, lanes(k)] = 1.0 - h * h
        return jnp.concatenate([high, low, high], axis=0)

    def forward(k, src, H1, H2, D1, D2, Xs):
        x = gather(src, k)
        x3 = split_q(x)
        Xs[:, lanes(k)] = x3[0 : 2 * QP]
        h13 = layer(k, x3, A1, H1, D1)
        return x, layer(k, h13, A2, H2, D2)

    def backward(k, D1, D2):
        g = gather(G, k)
        g3 = split_q(g)
        Gs[:, lanes(k)] = g3[0 : 2 * QP]
        high, low = split(dot(B3[...], g3) * D2[:, lanes(k)])
        GP2[0:hid, lanes(k)] = high
        GP2[hid : 2 * hid, lanes(k)] = low
        p3 = jnp.concatenate([high, low, high], axis=0)
        high, low = split(dot(B2[...], p3) * D1[:, lanes(k)])
        GP1[0:hid, lanes(k)] = high
        GP1[hid : 2 * hid, lanes(k)] = low
        p3 = jnp.concatenate([high, low, high], axis=0)
        return g, p3

    def weight_grads(H1, H2, Xs, start):
        def body(k, carry):
            m, i, o = carry
            m = m + dot_nt(H1[:, lanes(k)], GP2[:, lanes(k)])
            i = i + dot_nt(Xs[:, lanes(k)], GP1[:, lanes(k)])
            o = o + dot_nt(Gs[:, lanes(k)], H2[:, lanes(k)])
            return m, i, o

        return lax.fori_loop(0, steps, body, start)

    def propagate_back(g, from_left, from_right):
        own = S0[...] == 0
        for i in range(Q):
            o = reverse_index[i]
            if i < 5:
                src = from_right[i]
            elif i < 10:
                src = from_left[i - 5]
            else:
                src = g[i, 0:ny]
            moved = shifted(src, -offset_second[i], -offset_third[i])
            if i == 10:
                G[i, 0:ny] = g[i, 0:ny]
            else:
                G[i, 0:ny] = jnp.where(own, moved, 0.0) + jnp.where(S[o] == 0, 0.0, g[o, 0:ny])

    in_x.wait()

    def first(k):
        x, h23 = forward(k, X, H1a, H2a, D1a, D2a, Xa)
        scatter(U, k, x + dot(A3[...], h23))

        if k == 0:
            pl.semaphore_wait(barrier, n - 1)

            @pl.when(has_right)
            def _():
                sol_to_right().start()

            @pl.when(has_left)
            def _():
                sol_to_left().start()

        @pl.when(has_right)
        def _():
            col_to_right(k).start()

        @pl.when(has_left)
        def _():
            col_to_left(k).start()

    for k in range(steps):
        first(k)

    @pl.when(has_right)
    def _():
        cot_to_right().start()

    @pl.when(has_left)
    def _():
        cot_to_left().start()

    stack3(transposed(w_in[...], hid, tb.at[4]), hid, B1, tb.at[5])
    stack3(transposed(w_mid[...], hid, tb.at[6]), hid, B2, tb.at[7])
    stack3(w_out[...], QP, B3, tb.at[8])

    in_s.wait()

    @pl.when(has_left)
    def _():
        sol_to_right().wait_recv()

    @pl.when(has_right)
    def _():
        sol_to_left().wait_recv()

    for i in range(Q):
        plane = sol_l if i < 5 else sol_r if i < 10 else S0
        S[i] = shifted(plane[...], offset_second[i], offset_third[i])

    @pl.when(has_left)
    def _():
        for k in range(steps):
            col_to_right(k).wait_recv()

    @pl.when(has_right)
    def _():
        for k in range(steps):
            col_to_left(k).wait_recv()

    for i in range(Q):
        if i == 10:
            M[i, 0:ny] = U[i, 0:ny]
            continue
        src = col_l[i] if i < 5 else col_r[i - 5] if i < 10 else U[i, 0:ny]
        moved = shifted(src, offset_second[i], offset_third[i])
        M[i, 0:ny] = jnp.where(S[i] == 0, moved, U[reverse_index[i], 0:ny])

    def second(k, _):
        forward(k, M, H1b, H2b, D1b, D2b, Xb)
        return 0

    for k in range(steps):
        second(k, 0)

    in_c.wait()

    @pl.when(has_left)
    def _():
        cot_to_right().wait_recv()

    @pl.when(has_right)
    def _():
        cot_to_left().wait_recv()

    propagate_back(C, cot_l, cot_r)

    def third(k, _):
        g, p3 = backward(k, D1b, D2b)
        scatter(GM, k, g + dot(B1[...], p3))

        @pl.when(has_right)
        def _():
            gm_to_right(k).start()

        @pl.when(has_left)
        def _():
            gm_to_left(k).start()

        return 0

    for k in range(steps):
        third(k, 0)

    zero = (jnp.zeros((2 * hid, 2 * hid), f32), jnp.zeros((2 * QP, 2 * hid), f32), jnp.zeros((2 * QP, 2 * hid), f32))
    sums = weight_grads(H1b, H2b, Xb, zero)

    @pl.when(has_left)
    def _():
        for k in range(steps):
            gm_to_right(k).wait_recv()

    @pl.when(has_right)
    def _():
        for k in range(steps):
            gm_to_left(k).wait_recv()

    propagate_back(GM, gm_l, gm_r)

    @pl.when(has_right)
    def _():
        for k in range(steps):
            gm_to_right(k).wait_send()

    @pl.when(has_left)
    def _():
        for k in range(steps):
            gm_to_left(k).wait_send()

    def fourth(k, _):
        backward(k, D1a, D2a)
        return 0

    for k in range(steps):
        fourth(k, 0)

    sum_mid, sum_in, sum_out = weight_grads(H1a, H2a, Xa, sums)

    def folded(x):
        half = x.shape[0] // 2
        x = x[0:half] + x[half:]
        return x + pltpu.roll(x, hid, 1)

    pieces = []
    for whole in (folded(sum_mid), folded(sum_in), folded(sum_out)):
        pieces += [whole[j : j + 8] for j in range(0, whole.shape[0], 8)]
    per = share // 8
    for j in range(acc.shape[0] * per):
        piece = pieces[j] if j < len(pieces) else jnp.zeros((8, 128), f32)
        acc[j // per, (j % per) * 8 : (j % per) * 8 + 8] = piece

    inner = acc.shape[0]
    outer = n // inner
    mine, group = lax.rem(me, inner), me // inner
    first_of_group = group * inner

    def rs_copy(d):
        to = lax.rem(mine + d, inner)
        return remote(acc.at[to], rs.at[mine], rs_send.at[d], rs_recv.at[mine], first_of_group + to)

    def rs_arrival(d):
        source = lax.rem(mine + inner - d, inner)
        return remote(acc.at[mine], rs.at[source], rs_send.at[d], rs_recv.at[source], first_of_group + source)

    for d in range(1, inner):
        rs_copy(d).start()

    def fifth(k, _):
        rows = GP1[:, lanes(k)]
        scatter(GM, k, gather(G, k) + dot(B1[...], jnp.concatenate([rows, rows[0:hid]], axis=0)))
        return 0

    for k in range(steps):
        fifth(k, 0)
    out_x = pltpu.make_async_copy(GM.at[0:Q, 0:ny], out_pop, out_sem.at[0])
    out_x.start()

    total = acc[mine]
    for d in range(1, inner):
        rs_arrival(d).wait_recv()
        total = total + rs[lax.rem(mine + inner - d, inner)]
    across[group] = total

    def ac_copy(d):
        to = lax.rem(group + d, outer) * inner + mine
        return remote(across.at[group], across.at[group], ac_send.at[d], ac_recv.at[group], to)

    def ac_arrival(d):
        source = lax.rem(group + outer - d, outer)
        return remote(across.at[group], across.at[source], ac_send.at[d], ac_recv.at[source], source * inner + mine)

    for d in range(1, outer):
        ac_copy(d).start()
    for d in range(1, outer):
        ac_arrival(d).wait_recv()
    total = across[0]
    for j in range(1, outer):
        total = total + across[j]
    ag[mine] = total * factor

    def ag_copy(d):
        to = first_of_group + lax.rem(mine + d, inner)
        return remote(ag.at[mine], ag.at[mine], ag_send.at[d], ag_recv.at[mine], to)

    def ag_arrival(d):
        source = lax.rem(mine + inner - d, inner)
        return remote(ag.at[mine], ag.at[source], ag_send.at[d], ag_recv.at[source], first_of_group + source)

    for d in range(1, inner):
        ag_copy(d).start()
    for d in range(1, inner):
        ag_arrival(d).wait_recv()

    result = [ag[j // per, (j % per) * 8 : (j % per) * 8 + 8] for j in range(len(pieces))]
    count = hid // 8
    out_mid[...] = jnp.concatenate(result[0:count], axis=0)[:, 0:hid]
    out_in[...] = jnp.concatenate(result[count : count + 3], axis=0)[0:Q, 0:hid]
    last = jnp.concatenate(result[count + 3 :], axis=0)
    out_out[...] = last[0:Q, 0:hid]

    for d in range(1, inner):
        rs_copy(d).wait_send()
        ag_copy(d).wait_send()
    for d in range(1, outer):
        ac_copy(d).wait_send()

    @pl.when(has_right)
    def _():
        sol_to_right().wait_send()
        cot_to_right().wait_send()
        for k in range(steps):
            col_to_right(k).wait_send()

    @pl.when(has_left)
    def _():
        sol_to_left().wait_send()
        cot_to_left().wait_send()
        for k in range(steps):
            col_to_left(k).wait_send()

    out_x.wait()


def hand_on(*refs):
    n = (len(refs) - 2) // 3
    sources, targets, held = refs[:n], refs[n : 2 * n], refs[2 * n : 3 * n]
    in_sem, out_sem = refs[3 * n :]
    parts = [(sources[j], held[j], targets[j]) for j in range(1, n)]
    q = sources[0].shape[0]
    for at in range(0, q, 5):
        rows = pl.ds(at, min(5, q - at))
        parts.append((sources[0].at[rows], held[0].at[rows], targets[0].at[rows]))
    copies = [
        (pltpu.make_async_copy(a, b, in_sem.at[j]), pltpu.make_async_copy(b, c, out_sem.at[j]))
        for j, (a, b, c) in enumerate(parts)
    ]
    for one, _ in copies:
        one.start()
    for one, two in copies:
        one.wait()
        two.start()
    for _, two in copies:
        two.wait()


def per_device(n, populations, cotangent, solid_mask, weight_in, weight_mid, weight_out):
    q, nx, ny, nz = populations.shape
    hid = weight_mid.shape[0]
    voxels = ny * nz
    steps = ny // ROWS
    groups_of_8 = hid // 8 + 2 * (QP // 8)
    inner = math.gcd(n, 4)
    outer = n // inner
    share = 8 * -(-groups_of_8 // inner)
    factor = float(nx * voxels * n) ** (-0.5)
    plane = pltpu.VMEM((ny, nz), jnp.int32)
    planes = pltpu.VMEM((QP, ny + GAP, nz), f32)
    five = pltpu.VMEM((5, ny, nz), f32)
    stack = pltpu.VMEM((2 * hid, voxels), bf16)
    slope = pltpu.VMEM((hid, voxels), f32)
    thin = pltpu.VMEM((2 * QP, voxels), bf16)
    shares = pltpu.VMEM((inner, share, 128), f32)
    dma = pltpu.SemaphoreType.DMA
    grad, g_in, g_mid, g_out = pl.pallas_call(
        functools.partial(kernel, n, share, factor),
        out_shape=(
            jax.ShapeDtypeStruct((q, ny, nz), f32),
            jax.ShapeDtypeStruct(weight_in.shape, f32),
            jax.ShapeDtypeStruct(weight_mid.shape, f32),
            jax.ShapeDtypeStruct((q, hid), f32),
        ),
        in_specs=[pl.BlockSpec(memory_space=pl.ANY)] * 6,
        out_specs=(pl.BlockSpec(memory_space=pl.ANY),) + (pl.BlockSpec(memory_space=pltpu.VMEM),) * 3,
        scratch_shapes=[
            pltpu.VMEM((q, hid), f32), pltpu.VMEM((hid, hid), f32), pltpu.VMEM((q, hid), f32),
            planes, pltpu.VMEM((Q, ny, nz), f32), plane, planes, planes, planes, planes,
            pltpu.VMEM((Q, ny, nz), jnp.int32), plane, plane,
            five, five, five, five, five, five,
            stack, stack, slope, slope, thin,
            stack, stack, slope, slope, thin,
            stack, stack, thin,
            pltpu.VMEM((hid, KQ), bf16), pltpu.VMEM((hid, 3 * hid), bf16), pltpu.VMEM((QP, 3 * hid), bf16),
            pltpu.VMEM((QP, 3 * hid), bf16), pltpu.VMEM((hid, 3 * hid), bf16), pltpu.VMEM((hid, KQ), bf16),
            pltpu.VMEM((9, 256, 128), f32), shares, shares, pltpu.VMEM((outer, share, 128), f32), shares,
            dma((6,)), dma((1,)), dma((2,)), dma((2,)), dma((2,)), dma((2,)),
            dma((2, steps)), dma((2, steps)), dma((2, steps)), dma((2, steps)),
            dma((inner,)), dma((inner,)), dma((outer,)), dma((outer,)), dma((inner,)), dma((inner,)),
        ],
        compiler_params=pltpu.CompilerParams(
            collective_id=0, has_side_effects=True, vmem_limit_bytes=60 * 1024 * 1024
        ),
        name="lattice_backward",
    )(
        populations.reshape(q, ny, nz), cotangent.reshape(q, ny, nz), solid_mask.reshape(ny, nz),
        weight_in, weight_mid, weight_out.T,
    )
    results = (grad, g_in, g_mid, g_out)
    copies = len(results) - 1 + -(-q // 5)
    grad, g_in, g_mid, g_out = pl.pallas_call(
        hand_on,
        out_shape=tuple(jax.ShapeDtypeStruct(r.shape, r.dtype) for r in results),
        in_specs=[pl.BlockSpec(memory_space=pl.ANY)] * 4,
        out_specs=(pl.BlockSpec(memory_space=pl.ANY),) * 4,
        scratch_shapes=[pltpu.VMEM(r.shape, r.dtype) for r in results] + [dma((copies,)), dma((copies,))],
        name="hand_on",
    )(*results)
    return grad.reshape(populations.shape), g_in, g_mid, g_out.T


def solution(mesh):
    in_specs = (
        P(None, ("groups", "gx"), None, None),
        P(None, ("groups", "gx"), None, None),
        P(("groups", "gx"), None, None),
        P(),
        P(),
        P(),
    )
    out_specs = (
        P(None, ("groups", "gx"), None, None),
        P("groups", None),
        P("groups", None),
        P("groups", None),
    )
    return jax.shard_map(
        functools.partial(per_device, mesh.shape["gx"]),
        mesh=mesh, in_specs=in_specs, out_specs=out_specs, check_vma=False,
    )
```
